768 devices in a mesh: atm: 16 (over y, core), ocn: 48 (over x, z).
Axes of the slice: x: 4, y: 8, z: 12, core: 2. Of those that a mesh axis runs over, the one named last changes fastest.
Arguments:
- phys_flux: bfloat16 [192, 393216], P(None, ('atm', 'ocn')), may hold values from -6 to 6
- send_order: int32 [768, 512], P(('atm', 'ocn')), may hold values from 0 to 511, each once within a row
- near_src: int32 [12288], P(('atm', 'ocn')), may hold values from 0 to 3
- bil_src: int32 [12288, 4], P(('atm', 'ocn')), may hold values from 0 to 3
- nearest_w: bfloat16 [12288, 128, 128], P(('atm', 'ocn')), may hold values from -0.5 to 0.5
- bilinear_w: bfloat16 [12288, 4, 128, 128], P(('atm', 'ocn')), may hold values from -0.25 to 0.25
- owner_step: int32 [12288, 1], P(('atm', 'ocn')), may hold values from 0 to 4; in each aligned block of 16 rows (0 to 15, 16 to 31, ...) at most 4 rows name the same one
- slot: int32 [12288], P(('atm', 'ocn')), may hold values from 0 to 15
Outputs:
- remapped: bfloat16 [192, 1572864], P(None, ('atm', 'ocn'))
- ocean_flux: bfloat16 [12288, 48, 128], P(('atm', 'ocn'))
The draws below stay inside these ranges and needn't reach their ends.
Inputs may be any that keep to these rules, and one draw needn't show every extreme that they name: `send_order`: each device's row is an ordering of its 512 local columns. `owner_step`: among the 16 target blocks of one device, no value is named more than 4 times, a bound that some block reaches.
All inputs are finite; a program needn't handle non-finite values.
Results may differ from the reference program's by a relative error of at most 0.0044.
Values may be sent and summed in bfloat16 or wider, within the bound.
A program may use at most 32 MiB of HBM per device.

```python
import math
import jax
import jax.numpy as jnp
import numpy as np
from jax import lax

FIELDS = 48
SUB = 4
BLK = 128
NBIL = 4
NWIN = 5
COL_DEV = 512
TB = 16
OWN_BLK = 16
F = 192
NSB = 4
CAP = 4
DEVS = 768
NCOL = 393216
N_ATM = 16
N_OCN = 48


def plant(array, stream_key, low, largest):
    longest = array.shape.index(max(array.shape))
    spots = []
    for shift in (0, 1):
        where = [jax.random.randint(jax.random.fold_in(stream_key, axis), (), 0, length) for axis, length in enumerate(array.shape)]
        where[longest] = (where[longest] + shift) % array.shape[longest]
        spots.append(tuple(where))
    return array.at[spots[0]].set(low).at[spots[1]].set(largest)


def levels(stream_key, extent, cuts, low, largest):
    factor_of, own = 1.0, jax.random.fold_in(stream_key, 6)
    for dim, blocks in cuts:
        draws = jnp.exp(jax.random.uniform(jax.random.fold_in(own, dim), (blocks,), jnp.float32, low / len(cuts), largest / len(cuts)))
        factor_of = factor_of * jnp.repeat(draws, extent[dim] // blocks).reshape([-1 if axis == dim else 1 for axis in range(len(extent))])
    return factor_of


def routed_block(stream_key, own, number, rows, number_of, top, reach, skew):
    ranking = jax.random.permutation(stream_key, number_of)
    crowded, common = load_shares(number_of, rows * top, reach, skew, True), load_shares(number_of, rows * top, reach, skew, False)
    places = jnp.arange(number_of)

    def named(lengths, turn):
        used = int((lengths > 0).sum())
        fixed = max(1, used // 4)
        moved = fixed + (places - fixed + turn * (used - fixed)) % max(1, number_of - fixed)
        return jnp.zeros((number_of,), jnp.int32).at[ranking[jnp.where(places < fixed, places, moved)]].set(jnp.asarray(lengths, jnp.int32))

    lengths = jnp.where(number % 4 == 0, named(crowded, number // 4), named(common, number - number // 4 - 1))
    mixed = jax.random.permutation(jax.random.fold_in(own, 3), number_of)
    source_of, sink = mixed[0:number_of // 2 * 2:2], mixed[1:number_of // 2 * 2:2]
    margin = jnp.minimum(lengths[source_of] - 1, reach - lengths[sink]) // 2
    margin = jnp.where((source_of == ranking[0]) | (sink == ranking[0]) | (lengths[sink] == 0), 0, jnp.maximum(margin, 0))
    moved = jax.random.randint(jax.random.fold_in(own, 4), (number_of // 2,), 0, 1 << 20) % (margin + 1)
    lengths = lengths.at[source_of].add(-moved).at[sink].add(moved)
    labels = jnp.searchsorted(jnp.cumsum(lengths), jnp.arange(rows * top), side="right").astype(jnp.int32)
    table = labels.reshape(top, rows).T
    table = table[jax.random.permutation(jax.random.fold_in(own, 1), rows)]
    turn = jax.random.randint(jax.random.fold_in(own, 2), (rows, 1), 0, top)
    return jnp.take_along_axis(table, (jnp.arange(top)[None, :] + turn) % top, axis=1)


def load_shares(amount, total, reach, skew, full):
    weights = [(1 << 20) // math.isqrt(grade ** skew) + 1 for grade in range(1, amount + 1)]
    largest = reach if full else min(reach, max(-(-total // amount), total * weights[0] // sum(weights)))
    least = 1 if total - largest >= amount - 1 else 0
    counts, rest = [largest] + [least] * (amount - 1), total - largest - least * (amount - 1)
    while rest > 0:
        movable = [i for i in range(1, amount) if counts[i] < largest] or [i for i in range(1, amount) if counts[i] < reach]
        pool, budget = sum([weights[i] for i in movable]), rest
        for i in movable:
            addition = min(reach - counts[i], max(1, budget * weights[i] // pool), rest)
            counts[i] = counts[i] + addition
            rest = rest - addition
    return np.array(counts)


def centred(rng, dims, spread, most, cuts=(), held_as=jnp.bfloat16):
    entries = spread * jax.random.normal(rng, dims, jnp.float32)
    if cuts:
        entries = entries * levels(rng, dims, cuts, -0.22, 0.18)
    return jnp.clip(entries, -most, most).astype(held_as)


def setup_inputs(seed: int = 0) -> dict:
    splits = jax.random.split(jax.random.key(seed), 9)
    phys_flux = centred(splits[0], (F, NCOL), 1.0, 6.0, ((1, 768),))
    send_order = jax.vmap(lambda own: jax.random.permutation(own, COL_DEV))(jax.random.split(splits[1], DEVS)).reshape((DEVS, COL_DEV)).astype(jnp.int32)
    near_src = plant(jax.random.randint(splits[2], (DEVS * TB,), 0, NSB), jax.random.fold_in(splits[2], 1), 0, NSB - 1).astype(jnp.int32)
    bil_src = plant(jax.random.randint(splits[3], (DEVS * TB, NBIL), 0, NSB), jax.random.fold_in(splits[3], 1), 0, NSB - 1).astype(jnp.int32)
    nearest_w = centred(splits[4], (DEVS * TB, BLK, BLK), BLK ** -0.5, 0.5, ((0, 768),))
    bilinear_w = centred(splits[5], (DEVS * TB, NBIL, BLK, BLK), (NBIL * BLK) ** -0.5, 0.25, ((0, 768),))
    owner_step_keys = jax.random.split(jax.random.fold_in(splits[6], 1), (DEVS * TB) // TB)
    owner_step_turns = jax.random.permutation(jax.random.fold_in(splits[6], 3), (DEVS * TB) // TB)
    owner_step = jax.vmap(lambda own, number: routed_block(jax.random.fold_in(splits[6], 2), own, number, TB, NWIN, 1, CAP, 1))(owner_step_keys, owner_step_turns).reshape((DEVS * TB, 1))
    slot = plant(jax.random.randint(splits[7], (DEVS * TB,), 0, OWN_BLK), jax.random.fold_in(splits[7], 1), 0, OWN_BLK - 1).astype(jnp.int32)
    return {"phys_flux": phys_flux, "send_order": send_order, "near_src": near_src, "bil_src": bil_src, "nearest_w": nearest_w, "bilinear_w": bilinear_w, "owner_step": owner_step, "slot": slot}


def reference(phys_flux, send_order, near_src, bil_src, nearest_w, bilinear_w, owner_step, slot):
    devs = N_ATM * N_OCN
    width = COL_DEV // N_ATM
    half = F // 2
    phys4 = phys_flux.reshape(F, N_ATM, N_OCN, COL_DEV)
    order = send_order.reshape(N_ATM, N_OCN, COL_DEV)
    ordered = jnp.take_along_axis(phys4, order[None], axis=3)
    ordered = ordered.reshape(F, N_ATM, N_OCN, N_ATM, width).transpose(3, 2, 0, 1, 4)
    coupler = ordered.reshape(devs, F, COL_DEV)

    def one_device(items):
        cols, nsrc, bsrc, nwt, bwt = items
        blocks = cols.reshape(F, NSB, BLK).transpose(1, 0, 2)
        near = blocks[nsrc][:, :half].astype(jnp.float32)
        part_n = jnp.einsum("tfc,tcd->tfd", near, nwt.astype(jnp.float32))
        bil = blocks[bsrc][:, :, half:].astype(jnp.float32)
        part_b = jnp.einsum("tkfc,tkcd->tfd", bil, bwt.astype(jnp.float32))
        full = jnp.concatenate([part_n, part_b], axis=1)
        unit = jnp.mean(full.reshape(TB, FIELDS, SUB, BLK), axis=2)
        return full.astype(jnp.bfloat16), unit.astype(jnp.bfloat16)

    rem, units = lax.map(one_device, (coupler, near_src.reshape(devs, TB), bil_src.reshape(devs, TB, NBIL),
                                      nearest_w.reshape(devs, TB, BLK, BLK),
                                      bilinear_w.reshape(devs, TB, NBIL, BLK, BLK)))
    remapped = rem.transpose(2, 0, 1, 3).reshape(F, devs * TB * BLK)
    device_ids = jnp.repeat(jnp.arange(devs, dtype=jnp.int32), TB)
    own_idx = device_ids % N_OCN
    dest = (own_idx + owner_step[:, 0].astype(jnp.int32) - NWIN // 2 + N_OCN) % N_OCN
    target = ((device_ids // N_OCN) * N_OCN + dest) * OWN_BLK + slot.astype(jnp.int32)
    summed = jax.ops.segment_sum(units.reshape(devs * TB, FIELDS, BLK).astype(jnp.float32), target,
                                 num_segments=devs * OWN_BLK)
    return remapped, summed.astype(jnp.bfloat16)
```

```python
import functools

import jax
import jax.numpy as jnp
from jax import lax
from jax.experimental import pallas as pl
from jax.experimental.pallas import tpu as pltpu
from jax.sharding import PartitionSpec as P

SUB = 4
NWIN = 5
REACH = NWIN // 2
OWN_BLK = 16
CAP = 4
BLK = 128
ROWS = 192
HALF = 96
COLS = 512
TB = 16
N_ATM = 16
NSB = 4
NBIL = 4
LANES = 128
Q = 32
SEG = 64
GRP = 16
CHUNKS = ((1, 2), (0, 1))
MESH = pl.DeviceIdType.MESH
DISTANCES = (4, 3, 5, 2, 6, 1, 7, 0)
OFFSETS = (0, 4, 1, 3)
UNROLL = 4


def quarter_mask():
    return lax.broadcasted_iota(jnp.int32, (GRP, LANES), 1) // Q


def pick(quarter, values):
    out = values[3]
    for i in (2, 1, 0):
        out = jnp.where(quarter == i, values[i], out)
    return out


def kernel(
    phys, order, near_src, bil_src, near_w, bil_w, step, slot,
    remapped, ocean,
    phys_v, order_v, hot_v, near_wv, bil_wv, near_s, bil_s, step_s, slot_s,
    send_a, send_b, recv_a, recv_b, coupler, full_v, units_v, rem_v,
    pack_a, pack_b, got_a, got_b, slots_v, slots_g, ocean_v,
    in_sem, send_sem, recv_sem, usend_sem, urecv_sem, out_sem,
):
    a, o = lax.axis_index("atm"), lax.axis_index("ocn")
    n_ocn = lax.axis_size("ocn")
    n_chips = N_ATM // 2
    y, core = a // 2, a % 2

    def peer(distance, other):
        return ((y + distance) % n_chips) * 2 + (core + other) % 2

    partners = [(dy, x) for dy in DISTANCES for x in (0, 1) if (dy, x) != (0, 0)]

    def owner(index):
        return (o + (index - REACH) + n_ocn) % n_ocn

    barrier = pltpu.get_barrier_semaphore()
    for dy, x in partners:
        pl.semaphore_signal(barrier, inc=1, device_id=(peer(dy, x), o), device_id_type=MESH)
    for index in OFFSETS:
        pl.semaphore_signal(barrier, inc=1, device_id=(a, owner(index)), device_id_type=MESH)

    loads = [
        pltpu.make_async_copy(src, dst, in_sem.at[i])
        for i, (src, dst) in enumerate(
            [(order, order_v), (phys, phys_v), (step, step_s), (slot, slot_s), (near_src, near_s),
             (bil_src, bil_s), (bil_w, bil_wv), (near_w, near_wv)]
        )
    ]
    for load in loads:
        load.start()

    quarter = quarter_mask()
    loads[0].wait()
    for k in range(0, COLS, LANES):
        for n in range(0, COLS, LANES):
            index = jnp.broadcast_to(order_v[:, n:n + LANES], (LANES, LANES))
            rows = lax.broadcasted_iota(jnp.int32, (LANES, LANES), 0) + k
            hot_v[k:k + LANES, n:n + LANES] = jnp.where(index == rows, 1.0, 0.0).astype(jnp.bfloat16)
    loads[1].wait()
    turn = a % 4
    for chunk, (first, count), send in ((0, CHUNKS[0], send_a), (1, CHUNKS[1], send_b)):
        groups = [
            phys_v[pl.ds(pl.multiple_of((first + u) * SEG + ((q - turn + 4) % 4) * GRP, GRP), GRP), :]
            for u in range(count) for q in range(4)
        ]
        ordered = jnp.dot(jnp.concatenate(groups, axis=0), hot_v[...], preferred_element_type=jnp.float32)
        for u in range(count):
            for g in range(COLS // LANES):
                block = [
                    ordered[(u * 4 + q) * GRP:(u * 4 + q + 1) * GRP, g * LANES:(g + 1) * LANES]
                    for q in range(4)
                ]
                rolled = []
                for shift in range(4):
                    mixed = pick(quarter, [block[(e + shift) % 4] for e in range(4)])
                    rolled.append(pltpu.roll(mixed, shift * Q, 1) if shift else mixed)
                for e in range(4):
                    piece = pick(quarter, [rolled[(q - e) % 4] for q in range(4)])
                    send[g * 4 + e, u] = piece.astype(jnp.bfloat16)

    pl.semaphore_wait(barrier, len(partners) + len(OFFSETS))

    def piece_copy(chunk, dy, x):
        send, recv = ((send_a, recv_a), (send_b, recv_b))[chunk]
        d = peer(dy, x)
        lane = dy * 2 + x
        return pltpu.make_async_remote_copy(
            src_ref=send.at[d], dst_ref=recv.at[a],
            send_sem=send_sem.at[chunk, lane], recv_sem=recv_sem.at[chunk, lane],
            device_id=(d, o), device_id_type=MESH,
        )

    pieces = [[piece_copy(chunk, dy, x) for dy, x in partners] for chunk in range(2)]
    for chunk in range(2):
        for copy in pieces[chunk]:
            copy.start()
    recv_a[a] = send_a[a]
    recv_b[a] = send_b[a]

    for i in (2, 3):
        loads[i].wait()
    steps = [step_s[t] for t in range(TB)]
    places = []
    for t in range(TB):
        rank = jnp.int32(0)
        for before in range(t):
            rank = rank + jnp.where(steps[before] == steps[t], 1, 0)
        places.append(steps[t] * CAP + rank)
    source_of, slot_of = [], []
    for p in range(NWIN * CAP):
        t_of, slot_p = jnp.int32(0), jnp.int32(-1)
        for t in range(TB):
            t_of = jnp.where(places[t] == p, t, t_of)
            slot_p = jnp.where(places[t] == p, slot_s[t], slot_p)
        source_of.append(t_of)
        slot_of.append(slot_p)
    row = lax.broadcasted_iota(jnp.int32, (8, LANES), 0)
    for index in range(NWIN):
        tile = jnp.full((8, LANES), -1, jnp.int32)
        for rank in range(CAP):
            tile = jnp.where(row == rank, slot_of[index * CAP + rank], tile)
        slots_v[index] = tile

    def unit_copy(which, index):
        src, dst = ((pack_a, got_a), (pack_b, got_b), (slots_v, slots_g))[which]
        return pltpu.make_async_remote_copy(
            src_ref=src.at[index], dst_ref=dst.at[index],
            send_sem=usend_sem.at[which, index], recv_sem=urecv_sem.at[which, index],
            device_id=(a, owner(index)), device_id_type=MESH,
        )

    slot_copies = [unit_copy(2, index) for index in OFFSETS]
    for copy in slot_copies:
        copy.start()
    for i in range(4, 8):
        loads[i].wait()

    outs = []
    unit_copies = []
    for chunk, (first, count), recv, pack in (
        (0, CHUNKS[0], recv_a, pack_a), (1, CHUNKS[1], recv_b, pack_b)
    ):
        for copy in pieces[chunk]:
            copy.wait_recv()
        for b in range(NSB):
            for u in range(count):
                parts = [recv[b * 4 + s, u].astype(jnp.float32) for s in range(4)]
                groups = []
                for r in range(4):
                    mixed = pick(quarter, [parts[(q - r) % 4] for q in range(4)])
                    groups.append(pltpu.roll(mixed, (4 - r) * Q, 1) if r else mixed)
                start = (first + u) * SEG
                coupler[b, start:start + SEG, :] = jnp.concatenate(groups, axis=0).astype(jnp.bfloat16)
        low, high = first * SEG, (first + count) * SEG
        near_high, bil_low = min(high, HALF), max(low, HALF)
        fields = (high - low) // SUB

        def targets(i, carry):
            for j in range(UNROLL):
                t = i * UNROLL + j
                lane = pl.ds(pl.multiple_of(t * BLK, BLK), BLK)
                parts = []
                if low < near_high:
                    cells = coupler[near_s[t], low:near_high, :]
                    parts.append(jnp.dot(cells, near_wv[t], preferred_element_type=jnp.float32))
                if bil_low < high:
                    cells = jnp.concatenate(
                        [coupler[bil_s[k, t], bil_low:high, :] for k in range(NBIL)], axis=1
                    )
                    weights = bil_wv[t].reshape(NBIL * BLK, BLK)
                    parts.append(jnp.dot(cells, weights, preferred_element_type=jnp.float32))
                at = 0
                for part in parts:
                    full_v[t, low + at:low + at + part.shape[0], :] = part
                    rem_v[low + at:low + at + part.shape[0], lane] = part.astype(jnp.bfloat16)
                    at += part.shape[0]
                total = full_v[t, pl.ds(low, fields, stride=SUB), :]
                for s in range(1, SUB):
                    total = total + full_v[t, pl.ds(low + s, fields, stride=SUB), :]
                units_v[t, low // SUB:high // SUB, :] = (total * (1.0 / SUB)).astype(jnp.bfloat16)
            return carry

        lax.fori_loop(0, TB // UNROLL, targets, 0)
        for index in (*OFFSETS, REACH):
            for rank in range(CAP):
                pack[index, rank] = units_v[source_of[index * CAP + rank], low // SUB:high // SUB, :]
        copies = [unit_copy(chunk, index) for index in OFFSETS]
        for copy in copies:
            copy.start()
        unit_copies.append(copies)
        out = pltpu.make_async_copy(
            rem_v.at[pl.ds(low, high - low), :], remapped.at[pl.ds(low, high - low), :], out_sem.at[chunk]
        )
        out.start()
        outs.append(out)

    for copy in slot_copies:
        copy.wait_recv()
    for chunk, (first, count), pack, got in (
        (0, CHUNKS[0], pack_a, got_a), (1, CHUNKS[1], pack_b, got_b)
    ):
        low, high = first * SEG // SUB, (first + count) * SEG // SUB
        for copy in unit_copies[chunk]:
            copy.wait_recv()

        def blocks(i, carry):
            for part in range(low, high, GRP):
                sums = [jnp.zeros((GRP, LANES), jnp.float32) for _ in range(UNROLL)]
                for index in range(NWIN):
                    mine = index == REACH
                    for rank in range(CAP):
                        unit = (pack if mine else got)[index, rank, part - low:part - low + GRP, :]
                        unit = unit.astype(jnp.float32)
                        where = (slots_v if mine else slots_g)[index, rank:rank + 1, :]
                        where = jnp.broadcast_to(where, (GRP, LANES))
                        for j in range(UNROLL):
                            sums[j] = sums[j] + jnp.where(where == i * UNROLL + j, unit, 0.0)
                for j in range(UNROLL):
                    ocean_v[i * UNROLL + j, part:part + GRP, :] = sums[j].astype(jnp.bfloat16)
            return carry

        lax.fori_loop(0, OWN_BLK // UNROLL, blocks, 0)
        out = pltpu.make_async_copy(
            ocean_v.at[:, pl.ds(low, high - low), :], ocean.at[:, pl.ds(low, high - low), :],
            out_sem.at[2 + chunk],
        )
        out.start()
        outs.append(out)

    for group in (*pieces, *unit_copies, slot_copies):
        for copy in group:
            copy.wait_send()
    for out in outs:
        out.wait()


def local(phys_flux, send_order, near_src, bil_src, nearest_w, bilinear_w, owner_step, slot):
    any_space = pl.BlockSpec(memory_space=pl.ANY)
    bf16, f32, i32 = jnp.bfloat16, jnp.float32, jnp.int32
    fields = ROWS // SUB
    count_a, count_b = CHUNKS[0][1], CHUNKS[1][1]
    dma = pltpu.SemaphoreType.DMA
    return pl.pallas_call(
        kernel,
        out_shape=(
            jax.ShapeDtypeStruct((ROWS, TB * BLK), bf16),
            jax.ShapeDtypeStruct((OWN_BLK, fields, BLK), bf16),
        ),
        in_specs=[any_space] * 8,
        out_specs=(any_space, any_space),
        scratch_shapes=[
            pltpu.VMEM((ROWS, COLS), bf16),
            pltpu.VMEM((1, COLS), i32),
            pltpu.VMEM((COLS, COLS), bf16),
            pltpu.VMEM((TB, BLK, BLK), bf16),
            pltpu.VMEM((TB, NBIL, BLK, BLK), bf16),
            pltpu.SMEM((TB,), i32),
            pltpu.SMEM((NBIL, TB), i32),
            pltpu.SMEM((TB,), i32),
            pltpu.SMEM((TB,), i32),
            pltpu.VMEM((N_ATM, count_a, GRP, LANES), bf16),
            pltpu.VMEM((N_ATM, count_b, GRP, LANES), bf16),
            pltpu.VMEM((N_ATM, count_a, GRP, LANES), bf16),
            pltpu.VMEM((N_ATM, count_b, GRP, LANES), bf16),
            pltpu.VMEM((NSB, ROWS, BLK), bf16),
            pltpu.VMEM((TB, ROWS, BLK), f32),
            pltpu.VMEM((TB, fields, BLK), bf16),
            pltpu.VMEM((ROWS, TB * BLK), bf16),
            pltpu.VMEM((NWIN, CAP, count_a * GRP, LANES), bf16),
            pltpu.VMEM((NWIN, CAP, count_b * GRP, LANES), bf16),
            pltpu.VMEM((NWIN, CAP, count_a * GRP, LANES), bf16),
            pltpu.VMEM((NWIN, CAP, count_b * GRP, LANES), bf16),
            pltpu.VMEM((NWIN, 8, LANES), i32),
            pltpu.VMEM((NWIN, 8, LANES), i32),
            pltpu.VMEM((OWN_BLK, fields, BLK), bf16),
            dma((8,)),
            dma((2, N_ATM)),
            dma((2, N_ATM)),
            dma((3, NWIN)),
            dma((3, NWIN)),
            dma((4,)),
        ],
        compiler_params=pltpu.CompilerParams(
            collective_id=0, has_side_effects=True, vmem_limit_bytes=67043328
        ),
        name="coupler",
    )(
        phys_flux, send_order, near_src, bil_src.T, nearest_w, bilinear_w, owner_step.reshape(TB), slot
    )


def solution(mesh):
    placed = (
        P(None, ("atm", "ocn")),
        P(("atm", "ocn"), None),
        P(("atm", "ocn")),
        P(("atm", "ocn"), None),
        P(("atm", "ocn"), None, None),
        P(("atm", "ocn"), None, None, None),
        P(("atm", "ocn"), None),
        P(("atm", "ocn")),
    )
    return jax.shard_map(
        local,
        mesh=mesh,
        in_specs=placed,
        out_specs=(P(None, ("atm", "ocn")), P(("atm", "ocn"), None, None)),
        check_vma=False,
    )
```

```python
import functools

import jax
import jax.numpy as jnp
from jax import lax
from jax.experimental import pallas as pl
from jax.experimental.pallas import tpu as pltpu
from jax.sharding import PartitionSpec as P

SUB = 4
NWIN = 5
REACH = NWIN // 2
OWN_BLK = 16
CAP = 4
BLK = 128
ROWS = 192
HALF = 96
COLS = 512
TB = 16
N_ATM = 16
NSB = 4
NBIL = 4
LANES = 128
Q = 32
SEG = 64
GRP = 16
CHUNKS = (2, 1, 0)
MESH = pl.DeviceIdType.MESH
DISTANCES = (4, 3, 5, 2, 6, 1, 7, 0)
OFFSETS = (0, 4, 1, 3)
UNROLL = 4


def quarter_mask():
    return lax.broadcasted_iota(jnp.int32, (GRP, LANES), 1) // Q


def pick(quarter, values):
    out = values[3]
    for i in (2, 1, 0):
        out = jnp.where(quarter == i, values[i], out)
    return out


def kernel(
    phys, order, near_src, bil_src, near_w, bil_w, step, slot,
    remapped, ocean,
    phys_v, order_v, hot_v, near_wv, bil_wv, near_s, bil_s, step_s, slot_s,
    send, recv, coupler, full_v, units_v, pack, got, slots_v, slots_g,
    in_sem, send_sem, recv_sem, usend_sem, urecv_sem,
):
    a, o = lax.axis_index("atm"), lax.axis_index("ocn")
    n_ocn = lax.axis_size("ocn")
    n_chips = N_ATM // 2
    y, core = a // 2, a % 2

    def peer(distance, other):
        return ((y + distance) % n_chips) * 2 + (core + other) % 2

    partners = [(dy, x) for dy in DISTANCES for x in (0, 1) if (dy, x) != (0, 0)]

    def owner(index):
        return (o + (index - REACH) + n_ocn) % n_ocn

    barrier = pltpu.get_barrier_semaphore()
    for dy, x in partners:
        pl.semaphore_signal(barrier, inc=1, device_id=(peer(dy, x), o), device_id_type=MESH)
    for index in OFFSETS:
        pl.semaphore_signal(barrier, inc=1, device_id=(a, owner(index)), device_id_type=MESH)

    loads = [
        pltpu.make_async_copy(src, dst, in_sem.at[i])
        for i, (src, dst) in enumerate(
            [(order, order_v), (phys, phys_v), (step, step_s), (slot, slot_s), (near_src, near_s),
             (bil_src, bil_s), (bil_w, bil_wv), (near_w, near_wv)]
        )
    ]
    for load in loads:
        load.start()

    quarter = quarter_mask()
    loads[0].wait()
    for k in range(0, COLS, LANES):
        for n in range(0, COLS, LANES):
            index = jnp.broadcast_to(order_v[:, n:n + LANES], (LANES, LANES))
            rows = lax.broadcasted_iota(jnp.int32, (LANES, LANES), 0) + k
            hot_v[k:k + LANES, n:n + LANES] = jnp.where(index == rows, 1.0, 0.0).astype(jnp.bfloat16)
    loads[1].wait()
    turn = a % 4
    groups = [
        phys_v[pl.ds(pl.multiple_of(segment * SEG + ((q - turn + 4) % 4) * GRP, GRP), GRP), :]
        for segment in CHUNKS for q in range(4)
    ]
    ordered = jnp.dot(jnp.concatenate(groups, axis=0), hot_v[...], preferred_element_type=jnp.float32)
    for chunk in range(len(CHUNKS)):
        for g in range(COLS // LANES):
            block = [
                ordered[(chunk * 4 + q) * GRP:(chunk * 4 + q + 1) * GRP, g * LANES:(g + 1) * LANES]
                for q in range(4)
            ]
            rolled = []
            for shift in range(4):
                mixed = pick(quarter, [block[(e + shift) % 4] for e in range(4)])
                rolled.append(pltpu.roll(mixed, shift * Q, 1) if shift else mixed)
            for e in range(4):
                piece = pick(quarter, [rolled[(q - e) % 4] for q in range(4)])
                send[chunk, g * 4 + e] = piece.astype(jnp.bfloat16)

    pl.semaphore_wait(barrier, len(partners) + len(OFFSETS))

    def piece_copy(chunk, dy, x):
        d = peer(dy, x)
        lane = dy * 2 + x
        return pltpu.make_async_remote_copy(
            src_ref=send.at[chunk, d], dst_ref=recv.at[chunk, a],
            send_sem=send_sem.at[chunk, lane], recv_sem=recv_sem.at[chunk, lane],
            device_id=(d, o), device_id_type=MESH,
        )

    pieces = [[piece_copy(chunk, dy, x) for dy, x in partners] for chunk in range(len(CHUNKS))]
    for group in pieces:
        for copy in group:
            copy.start()
    for chunk in range(len(CHUNKS)):
        recv[chunk, a] = send[chunk, a]

    for i in (2, 3):
        loads[i].wait()
    steps = [step_s[t] for t in range(TB)]
    places = []
    for t in range(TB):
        rank = jnp.int32(0)
        for before in range(t):
            rank = rank + jnp.where(steps[before] == steps[t], 1, 0)
        places.append(steps[t] * CAP + rank)
    source_of, slot_of = [], []
    for p in range(NWIN * CAP):
        t_of, slot_p = jnp.int32(0), jnp.int32(-1)
        for t in range(TB):
            t_of = jnp.where(places[t] == p, t, t_of)
            slot_p = jnp.where(places[t] == p, slot_s[t], slot_p)
        source_of.append(t_of)
        slot_of.append(slot_p)
    row = lax.broadcasted_iota(jnp.int32, (8, LANES), 0)
    for index in range(NWIN):
        tile = jnp.full((8, LANES), -1, jnp.int32)
        for rank in range(CAP):
            tile = jnp.where(row == rank, slot_of[index * CAP + rank], tile)
        slots_v[index] = tile

    def owner_copy(src, dst, which, index):
        return pltpu.make_async_remote_copy(
            src_ref=src, dst_ref=dst,
            send_sem=usend_sem.at[which, index], recv_sem=urecv_sem.at[which, index],
            device_id=(a, owner(index)), device_id_type=MESH,
        )

    slot_copies = [owner_copy(slots_v.at[i], slots_g.at[i], len(CHUNKS), i) for i in OFFSETS]
    for copy in slot_copies:
        copy.start()
    for i in range(4, 8):
        loads[i].wait()

    unit_copies = []
    for chunk, segment in enumerate(CHUNKS):
        for copy in pieces[chunk]:
            copy.wait_recv()
        low, high = segment * SEG, (segment + 1) * SEG
        for b in range(NSB):
            parts = [recv[chunk, b * 4 + s].astype(jnp.float32) for s in range(4)]
            groups = []
            for r in range(4):
                mixed = pick(quarter, [parts[(q - r) % 4] for q in range(4)])
                groups.append(pltpu.roll(mixed, (4 - r) * Q, 1) if r else mixed)
            coupler[b, low:high, :] = jnp.concatenate(groups, axis=0).astype(jnp.bfloat16)
        near_high, bil_low = min(high, HALF), max(low, HALF)
        fields = SEG // SUB

        def targets(i, carry):
            for j in range(UNROLL):
                t = i * UNROLL + j
                lane = pl.ds(pl.multiple_of(t * BLK, BLK), BLK)
                parts = []
                if low < near_high:
                    cells = coupler[near_s[t], low:near_high, :]
                    parts.append(jnp.dot(cells, near_wv[t], preferred_element_type=jnp.float32))
                if bil_low < high:
                    cells = jnp.concatenate(
                        [coupler[bil_s[k, t], bil_low:high, :] for k in range(NBIL)], axis=1
                    )
                    weights = bil_wv[t].reshape(NBIL * BLK, BLK)
                    parts.append(jnp.dot(cells, weights, preferred_element_type=jnp.float32))
                at = 0
                for part in parts:
                    full_v[t, low + at:low + at + part.shape[0], :] = part
                    remapped[low + at:low + at + part.shape[0], lane] = part.astype(jnp.bfloat16)
                    at += part.shape[0]
                total = full_v[t, pl.ds(low, fields, stride=SUB), :]
                for s in range(1, SUB):
                    total = total + full_v[t, pl.ds(low + s, fields, stride=SUB), :]
                units_v[t, low // SUB:high // SUB, :] = (total * (1.0 / SUB)).astype(jnp.bfloat16)
            return carry

        lax.fori_loop(0, TB // UNROLL, targets, 0)
        for index in (*OFFSETS, REACH):
            for rank in range(CAP):
                pack[chunk, index, rank] = units_v[source_of[index * CAP + rank], low // SUB:high // SUB, :]
        copies = [owner_copy(pack.at[chunk, i], got.at[chunk, i], chunk, i) for i in OFFSETS]
        for copy in copies:
            copy.start()
        unit_copies.append(copies)

    for copy in slot_copies:
        copy.wait_recv()
    for chunk, segment in enumerate(CHUNKS):
        low = segment * GRP
        for copy in unit_copies[chunk]:
            copy.wait_recv()

        def blocks(i, carry):
            sums = [jnp.zeros((GRP, LANES), jnp.float32) for _ in range(UNROLL)]
            for index in range(NWIN):
                mine = index == REACH
                for rank in range(CAP):
                    unit = (pack if mine else got)[chunk, index, rank].astype(jnp.float32)
                    where = (slots_v if mine else slots_g)[index, rank:rank + 1, :]
                    where = jnp.broadcast_to(where, (GRP, LANES))
                    for j in range(UNROLL):
                        sums[j] = sums[j] + jnp.where(where == i * UNROLL + j, unit, 0.0)
            for j in range(UNROLL):
                ocean[i * UNROLL + j, low:low + GRP, :] = sums[j].astype(jnp.bfloat16)
            return carry

        lax.fori_loop(0, OWN_BLK // UNROLL, blocks, 0)

    for group in (*pieces, *unit_copies, slot_copies):
        for copy in group:
            copy.wait_send()


def write(remapped, ocean, remapped_out, ocean_out, sem):
    copies = [
        pltpu.make_async_copy(remapped, remapped_out, sem.at[0]),
        pltpu.make_async_copy(ocean, ocean_out, sem.at[1]),
    ]
    for copy in copies:
        copy.start()
    for copy in copies:
        copy.wait()


def local(phys_flux, send_order, near_src, bil_src, nearest_w, bilinear_w, owner_step, slot):
    bf16, f32, i32 = jnp.bfloat16, jnp.float32, jnp.int32
    fields, chunks = ROWS // SUB, len(CHUNKS)
    dma = pltpu.SemaphoreType.DMA
    hbm = pl.BlockSpec(memory_space=pltpu.HBM)
    vmem = pl.BlockSpec(memory_space=pltpu.VMEM)
    args = (
        phys_flux, send_order, near_src, bil_src.T, nearest_w, bilinear_w, owner_step.reshape(TB), slot
    )
    results = pl.pallas_call(
        kernel,
        out_shape=(
            pltpu.VMEM((ROWS, TB * BLK), bf16),
            pltpu.VMEM((OWN_BLK, fields, BLK), bf16),
        ),
        in_specs=[hbm] * 8,
        out_specs=(vmem, vmem),
        scratch_shapes=[
            pltpu.VMEM((ROWS, COLS), bf16),
            pltpu.VMEM((1, COLS), i32),
            pltpu.VMEM((COLS, COLS), bf16),
            pltpu.VMEM((TB, BLK, BLK), bf16),
            pltpu.VMEM((TB, NBIL, BLK, BLK), bf16),
            pltpu.SMEM((TB,), i32),
            pltpu.SMEM((NBIL, TB), i32),
            pltpu.SMEM((TB,), i32),
            pltpu.SMEM((TB,), i32),
            pltpu.VMEM((chunks, N_ATM, GRP, LANES), bf16),
            pltpu.VMEM((chunks, N_ATM, GRP, LANES), bf16),
            pltpu.VMEM((NSB, ROWS, BLK), bf16),
            pltpu.VMEM((TB, ROWS, BLK), f32),
            pltpu.VMEM((TB, fields, BLK), bf16),
            pltpu.VMEM((chunks, NWIN, CAP, GRP, LANES), bf16),
            pltpu.VMEM((chunks, NWIN, CAP, GRP, LANES), bf16),
            pltpu.VMEM((NWIN, 8, LANES), i32),
            pltpu.VMEM((NWIN, 8, LANES), i32),
            dma((8,)),
            dma((chunks, N_ATM)),
            dma((chunks, N_ATM)),
            dma((chunks + 1, NWIN)),
            dma((chunks + 1, NWIN)),
        ],
        compiler_params=pltpu.CompilerParams(
            collective_id=0, has_side_effects=True, vmem_limit_bytes=24 << 20
        ),
        name="coupler",
    )(*[pltpu.with_memory_space_constraint(x, pltpu.HBM) for x in args])
    return pl.pallas_call(
        write,
        out_shape=(
            pltpu.HBM((ROWS, TB * BLK), bf16),
            pltpu.HBM((OWN_BLK, fields, BLK), bf16),
        ),
        in_specs=[vmem, vmem],
        out_specs=(hbm, hbm),
        scratch_shapes=[dma((2,))],
        compiler_params=pltpu.CompilerParams(vmem_limit_bytes=1 << 20),
        name="write",
    )(*[pltpu.with_memory_space_constraint(x, pltpu.VMEM) for x in results])


def solution(mesh):
    placed = (
        P(None, ("atm", "ocn")),
        P(("atm", "ocn"), None),
        P(("atm", "ocn")),
        P(("atm", "ocn"), None),
        P(("atm", "ocn"), None, None),
        P(("atm", "ocn"), None, None, None),
        P(("atm", "ocn"), None),
        P(("atm", "ocn")),
    )
    return jax.shard_map(
        local,
        mesh=mesh,
        in_specs=placed,
        out_specs=(P(None, ("atm", "ocn")), P(("atm", "ocn"), None, None)),
        check_vma=False,
    )
```

```python
import functools

import jax
import jax.numpy as jnp
from jax import lax
from jax.experimental import pallas as pl
from jax.experimental.pallas import tpu as pltpu
from jax.sharding import PartitionSpec as P

SUB = 4
NWIN = 5
REACH = NWIN // 2
OWN_BLK = 16
CAP = 4
BLK = 128
ROWS = 192
HALF = 96
COLS = 512
TB = 16
N_ATM = 16
NSB = 4
NBIL = 4
LANES = 128
Q = 32
SEG = 64
GRP = 16
CHUNKS = (2, 1, 0)
MESH = pl.DeviceIdType.MESH
DISTANCES = (4, 3, 5, 2, 6, 1, 7, 0)
OFFSETS = (0, 4, 1, 3)
UNROLL = 4


def quarter_mask():
    return lax.broadcasted_iota(jnp.int32, (GRP, LANES), 1) // Q


def pick(quarter, values):
    out = values[3]
    for i in (2, 1, 0):
        out = jnp.where(quarter == i, values[i], out)
    return out


def kernel(
    phys, order, near_src, bil_src, near_w, bil_w, step, slot,
    remapped, ocean,
    phys_v, order_v, hot_v, near_wv, bil_wv, near_s, bil_s, step_s, slot_s,
    send, recv, coupler, full_v, units_v, pack, got, slots_v, slots_g, total_v,
    in_sem, send_sem, recv_sem, usend_sem, urecv_sem,
):
    a, o = lax.axis_index("atm"), lax.axis_index("ocn")
    n_ocn = lax.axis_size("ocn")
    n_chips = N_ATM // 2
    y, core = a // 2, a % 2

    def peer(distance, other):
        return ((y + distance) % n_chips) * 2 + (core + other) % 2

    partners = [(dy, x) for dy in DISTANCES for x in (0, 1) if (dy, x) != (0, 0)]

    def owner(index):
        return (o + (index - REACH) + n_ocn) % n_ocn

    barrier = pltpu.get_barrier_semaphore()
    for dy, x in partners:
        pl.semaphore_signal(barrier, inc=1, device_id=(peer(dy, x), o), device_id_type=MESH)
    for index in OFFSETS:
        pl.semaphore_signal(barrier, inc=1, device_id=(a, owner(index)), device_id_type=MESH)

    loads = [
        pltpu.make_async_copy(src, dst, in_sem.at[i])
        for i, (src, dst) in enumerate(
            [(order, order_v), (phys, phys_v), (step, step_s), (slot, slot_s), (near_src, near_s),
             (bil_src, bil_s), (bil_w, bil_wv), (near_w, near_wv)]
        )
    ]
    for load in loads:
        load.start()

    quarter = quarter_mask()
    loads[0].wait()
    for k in range(0, COLS, LANES):
        for n in range(0, COLS, LANES):
            index = jnp.broadcast_to(order_v[:, n:n + LANES], (LANES, LANES))
            rows = lax.broadcasted_iota(jnp.int32, (LANES, LANES), 0) + k
            hot_v[k:k + LANES, n:n + LANES] = jnp.where(index == rows, 1.0, 0.0).astype(jnp.bfloat16)
    loads[1].wait()
    turn = a % 4
    groups = [
        phys_v[pl.ds(pl.multiple_of(segment * SEG + ((q - turn + 4) % 4) * GRP, GRP), GRP), :]
        for segment in CHUNKS for q in range(4)
    ]
    ordered = jnp.dot(jnp.concatenate(groups, axis=0), hot_v[...], preferred_element_type=jnp.float32)
    for chunk in range(len(CHUNKS)):
        for g in range(COLS // LANES):
            block = [
                ordered[(chunk * 4 + q) * GRP:(chunk * 4 + q + 1) * GRP, g * LANES:(g + 1) * LANES]
                for q in range(4)
            ]
            rolled = []
            for shift in range(4):
                mixed = pick(quarter, [block[(e + shift) % 4] for e in range(4)])
                rolled.append(pltpu.roll(mixed, shift * Q, 1) if shift else mixed)
            for e in range(4):
                piece = pick(quarter, [rolled[(q - e) % 4] for q in range(4)])
                send[chunk, g * 4 + e] = piece.astype(jnp.bfloat16)

    pl.semaphore_wait(barrier, len(partners) + len(OFFSETS))

    def piece_copy(chunk, dy, x):
        d = peer(dy, x)
        lane = dy * 2 + x
        return pltpu.make_async_remote_copy(
            src_ref=send.at[chunk, d], dst_ref=recv.at[chunk, a],
            send_sem=send_sem.at[chunk, lane], recv_sem=recv_sem.at[chunk, lane],
            device_id=(d, o), device_id_type=MESH,
        )

    pieces = [[piece_copy(chunk, dy, x) for dy, x in partners] for chunk in range(len(CHUNKS))]
    for group in pieces:
        for copy in group:
            copy.start()
    for chunk in range(len(CHUNKS)):
        recv[chunk, a] = send[chunk, a]

    for i in (2, 3):
        loads[i].wait()
    steps = [step_s[t] for t in range(TB)]
    places = []
    for t in range(TB):
        rank = jnp.int32(0)
        for before in range(t):
            rank = rank + jnp.where(steps[before] == steps[t], 1, 0)
        places.append(steps[t] * CAP + rank)
    source_of, slot_of = [], []
    for p in range(NWIN * CAP):
        t_of, slot_p = jnp.int32(0), jnp.int32(-1)
        for t in range(TB):
            t_of = jnp.where(places[t] == p, t, t_of)
            slot_p = jnp.where(places[t] == p, slot_s[t], slot_p)
        source_of.append(t_of)
        slot_of.append(slot_p)
    row = lax.broadcasted_iota(jnp.int32, (8, LANES), 0)
    for index in range(NWIN):
        tile = jnp.full((8, LANES), -1, jnp.int32)
        for rank in range(CAP):
            tile = jnp.where(row == rank, slot_of[index * CAP + rank], tile)
        slots_v[index] = tile

    def owner_copy(src, dst, which, index):
        return pltpu.make_async_remote_copy(
            src_ref=src, dst_ref=dst,
            send_sem=usend_sem.at[which, index], recv_sem=urecv_sem.at[which, index],
            device_id=(a, owner(index)), device_id_type=MESH,
        )

    slot_copies = [owner_copy(slots_v.at[i], slots_g.at[i], len(CHUNKS), i) for i in OFFSETS]
    for copy in slot_copies:
        copy.start()
    for i in range(4, 8):
        loads[i].wait()

    unit_copies = []
    for chunk, segment in enumerate(CHUNKS):
        for copy in pieces[chunk]:
            copy.wait_recv()
        low, high = segment * SEG, (segment + 1) * SEG
        for b in range(NSB):
            parts = [recv[chunk, b * 4 + s].astype(jnp.float32) for s in range(4)]
            groups = []
            for r in range(4):
                mixed = pick(quarter, [parts[(q - r) % 4] for q in range(4)])
                groups.append(pltpu.roll(mixed, (4 - r) * Q, 1) if r else mixed)
            coupler[b, low:high, :] = jnp.concatenate(groups, axis=0).astype(jnp.bfloat16)
        near_high, bil_low = min(high, HALF), max(low, HALF)
        fields = SEG // SUB

        def targets():
            for t in range(TB):
                lane = slice(t * BLK, (t + 1) * BLK)
                parts = []
                if low < near_high:
                    cells = coupler[near_s[t], low:near_high, :]
                    parts.append(jnp.dot(cells, near_wv[t], preferred_element_type=jnp.float32))
                if bil_low < high:
                    cells = jnp.concatenate(
                        [coupler[bil_s[k, t], bil_low:high, :] for k in range(NBIL)], axis=1
                    )
                    weights = bil_wv[t].reshape(NBIL * BLK, BLK)
                    parts.append(jnp.dot(cells, weights, preferred_element_type=jnp.float32))
                at = 0
                for part in parts:
                    full_v[t, low + at:low + at + part.shape[0], :] = part
                    remapped[low + at:low + at + part.shape[0], lane] = part.astype(jnp.bfloat16)
                    at += part.shape[0]
                total = full_v[t, pl.ds(low, fields, stride=SUB), :]
                for s in range(1, SUB):
                    total = total + full_v[t, pl.ds(low + s, fields, stride=SUB), :]
                units_v[t, low // SUB:high // SUB, :] = (total * (1.0 / SUB)).astype(jnp.bfloat16)

        targets()
        for index in (*OFFSETS, REACH):
            for rank in range(CAP):
                pack[chunk, index, rank] = units_v[source_of[index * CAP + rank], low // SUB:high // SUB, :]
        copies = [owner_copy(pack.at[chunk, i], got.at[chunk, i], chunk, i) for i in OFFSETS]
        for copy in copies:
            copy.start()
        unit_copies.append(copies)

    for copy in slot_copies:
        copy.wait_recv()
    for chunk, segment in enumerate(CHUNKS):
        low = segment * GRP
        for stage, indices in enumerate(((2, 1, 3), (0, 4))):
            for copy, index in zip(unit_copies[chunk], OFFSETS):
                if index in indices:
                    copy.wait_recv()
            for first in range(0, OWN_BLK, UNROLL):
                wanted = range(first, first + UNROLL)
                sums = [total_v[i] if stage else jnp.zeros((GRP, LANES), jnp.float32) for i in wanted]
                for index in indices:
                    mine = index == REACH
                    for rank in range(CAP):
                        unit = (pack if mine else got)[chunk, index, rank].astype(jnp.float32)
                        where = (slots_v if mine else slots_g)[index, rank:rank + 1, :]
                        where = jnp.broadcast_to(where, (GRP, LANES))
                        for j, i in enumerate(wanted):
                            sums[j] = sums[j] + jnp.where(where == i, unit, 0.0)
                for j, i in enumerate(wanted):
                    if stage:
                        ocean[i, low:low + GRP, :] = sums[j].astype(jnp.bfloat16)
                    else:
                        total_v[i] = sums[j]

    for group in (*pieces, *unit_copies, slot_copies):
        for copy in group:
            copy.wait_send()


def write(remapped, ocean, remapped_out, ocean_out, sem):
    copies = [
        pltpu.make_async_copy(remapped, remapped_out, sem.at[0]),
        pltpu.make_async_copy(ocean, ocean_out, sem.at[1]),
    ]
    for copy in copies:
        copy.start()
    for copy in copies:
        copy.wait()


def local(phys_flux, send_order, near_src, bil_src, nearest_w, bilinear_w, owner_step, slot):
    bf16, f32, i32 = jnp.bfloat16, jnp.float32, jnp.int32
    fields, chunks = ROWS // SUB, len(CHUNKS)
    dma = pltpu.SemaphoreType.DMA
    hbm = pl.BlockSpec(memory_space=pltpu.HBM)
    vmem = pl.BlockSpec(memory_space=pltpu.VMEM)
    args = (
        phys_flux, send_order, near_src, bil_src.T, nearest_w, bilinear_w, owner_step.reshape(TB), slot
    )
    results = pl.pallas_call(
        kernel,
        out_shape=(
            pltpu.VMEM((ROWS, TB * BLK), bf16),
            pltpu.VMEM((OWN_BLK, fields, BLK), bf16),
        ),
        in_specs=[hbm] * 8,
        out_specs=(vmem, vmem),
        scratch_shapes=[
            pltpu.VMEM((ROWS, COLS), bf16),
            pltpu.VMEM((1, COLS), i32),
            pltpu.VMEM((COLS, COLS), bf16),
            pltpu.VMEM((TB, BLK, BLK), bf16),
            pltpu.VMEM((TB, NBIL, BLK, BLK), bf16),
            pltpu.SMEM((TB,), i32),
            pltpu.SMEM((NBIL, TB), i32),
            pltpu.SMEM((TB,), i32),
            pltpu.SMEM((TB,), i32),
            pltpu.VMEM((chunks, N_ATM, GRP, LANES), bf16),
            pltpu.VMEM((chunks, N_ATM, GRP, LANES), bf16),
            pltpu.VMEM((NSB, ROWS, BLK), bf16),
            pltpu.VMEM((TB, ROWS, BLK), f32),
            pltpu.VMEM((TB, fields, BLK), bf16),
            pltpu.VMEM((chunks, NWIN, CAP, GRP, LANES), bf16),
            pltpu.VMEM((chunks, NWIN, CAP, GRP, LANES), bf16),
            pltpu.VMEM((NWIN, 8, LANES), i32),
            pltpu.VMEM((NWIN, 8, LANES), i32),
            pltpu.VMEM((OWN_BLK, GRP, LANES), f32),
            dma((8,)),
            dma((chunks, N_ATM)),
            dma((chunks, N_ATM)),
            dma((chunks + 1, NWIN)),
            dma((chunks + 1, NWIN)),
        ],
        compiler_params=pltpu.CompilerParams(
            collective_id=0, has_side_effects=True, vmem_limit_bytes=24 << 20
        ),
        name="coupler",
    )(*[pltpu.with_memory_space_constraint(x, pltpu.HBM) for x in args])
    return pl.pallas_call(
        write,
        out_shape=(
            pltpu.HBM((ROWS, TB * BLK), bf16),
            pltpu.HBM((OWN_BLK, fields, BLK), bf16),
        ),
        in_specs=[vmem, vmem],
        out_specs=(hbm, hbm),
        scratch_shapes=[dma((2,))],
        compiler_params=pltpu.CompilerParams(vmem_limit_bytes=1 << 20),
        name="write",
    )(*[pltpu.with_memory_space_constraint(x, pltpu.VMEM) for x in results])


def solution(mesh):
    placed = (
        P(None, ("atm", "ocn")),
        P(("atm", "ocn"), None),
        P(("atm", "ocn")),
        P(("atm", "ocn"), None),
        P(("atm", "ocn"), None, None),
        P(("atm", "ocn"), None, None, None),
        P(("atm", "ocn"), None),
        P(("atm", "ocn")),
    )
    return jax.shard_map(
        local,
        mesh=mesh,
        in_specs=placed,
        out_specs=(P(None, ("atm", "ocn")), P(("atm", "ocn"), None, None)),
        check_vma=False,
    )
```

```python
import functools

import jax
import jax.numpy as jnp
from jax import lax
from jax.experimental import pallas as pl
from jax.experimental.pallas import tpu as pltpu
from jax.sharding import PartitionSpec as P

SUB = 4
NWIN = 5
REACH = NWIN // 2
OWN_BLK = 16
CAP = 4
BLK = 128
ROWS = 192
HALF = 96
COLS = 512
TB = 16
N_ATM = 16
NSB = 4
NBIL = 4
LANES = 128
Q = 32
SEG = 64
GRP = 16
CHUNKS = (2, 1, 0)
MESH = pl.DeviceIdType.MESH
DISTANCES = (4, 3, 5, 2, 6, 1, 7, 0)
OFFSETS = (0, 4, 1, 3)
UNROLL = 4


def quarter_mask():
    return lax.broadcasted_iota(jnp.int32, (GRP, LANES), 1) // Q


def pick(quarter, values):
    out = values[3]
    for i in (2, 1, 0):
        out = jnp.where(quarter == i, values[i], out)
    return out


def kernel(
    phys, order, near_src, bil_src, near_w, bil_w, step, slot,
    remapped, ocean,
    phys_v, order_v, hot_v, near_wv, bil_wv, near_s, bil_s, step_s, slot_s,
    send, recv, coupler, full_v, units_v, pack, got, slots_v, slots_g, total_v,
    in_sem, send_sem, recv_sem, usend_sem, urecv_sem,
):
    a, o = lax.axis_index("atm"), lax.axis_index("ocn")
    n_ocn = lax.axis_size("ocn")
    n_chips = N_ATM // 2
    y, core = a // 2, a % 2

    def peer(distance, other):
        return ((y + distance) % n_chips) * 2 + (core + other) % 2

    partners = [(dy, x) for dy in DISTANCES for x in (0, 1) if (dy, x) != (0, 0)]

    def owner(index):
        return (o + (index - REACH) + n_ocn) % n_ocn

    barrier = pltpu.get_barrier_semaphore()
    for dy, x in partners:
        pl.semaphore_signal(barrier, inc=1, device_id=(peer(dy, x), o), device_id_type=MESH)
    for index in OFFSETS:
        pl.semaphore_signal(barrier, inc=1, device_id=(a, owner(index)), device_id_type=MESH)

    loads = [
        pltpu.make_async_copy(src, dst, in_sem.at[i])
        for i, (src, dst) in enumerate(
            [(order, order_v), (phys, phys_v), (step, step_s), (slot, slot_s), (near_src, near_s),
             (bil_src, bil_s), (bil_w, bil_wv), (near_w, near_wv)]
        )
    ]
    for load in loads:
        load.start()

    quarter = quarter_mask()
    loads[0].wait()
    for k in range(0, COLS, LANES):
        for n in range(0, COLS, LANES):
            index = jnp.broadcast_to(order_v[:, n:n + LANES], (LANES, LANES))
            rows = lax.broadcasted_iota(jnp.int32, (LANES, LANES), 0) + k
            hot_v[k:k + LANES, n:n + LANES] = jnp.where(index == rows, 1.0, 0.0).astype(jnp.bfloat16)
    loads[1].wait()
    turn = a % 4

    def arrange(chunk):
        start = CHUNKS[chunk] * SEG
        groups = [
            phys_v[pl.ds(pl.multiple_of(start + ((q - turn + 4) % 4) * GRP, GRP), GRP), :] for q in range(4)
        ]
        ordered = jnp.dot(jnp.concatenate(groups, axis=0), hot_v[...], preferred_element_type=jnp.float32)
        for g in range(COLS // LANES):
            block = [ordered[q * GRP:(q + 1) * GRP, g * LANES:(g + 1) * LANES] for q in range(4)]
            rolled = []
            for shift in range(4):
                mixed = pick(quarter, [block[(e + shift) % 4] for e in range(4)])
                rolled.append(pltpu.roll(mixed, shift * Q, 1) if shift else mixed)
            for e in range(4):
                piece = pick(quarter, [rolled[(q - e) % 4] for q in range(4)])
                send[chunk, g * 4 + e] = piece.astype(jnp.bfloat16)

    arrange(0)
    pl.semaphore_wait(barrier, len(partners) + len(OFFSETS))

    def piece_copy(chunk, dy, x):
        d = peer(dy, x)
        lane = dy * 2 + x
        return pltpu.make_async_remote_copy(
            src_ref=send.at[chunk, d], dst_ref=recv.at[chunk, a],
            send_sem=send_sem.at[chunk, lane], recv_sem=recv_sem.at[chunk, lane],
            device_id=(d, o), device_id_type=MESH,
        )

    pieces = [[piece_copy(chunk, dy, x) for dy, x in partners] for chunk in range(len(CHUNKS))]
    for chunk, group in enumerate(pieces):
        if chunk:
            arrange(chunk)
        for copy in group:
            copy.start()
    for chunk in range(len(CHUNKS)):
        recv[chunk, a] = send[chunk, a]

    for i in (2, 3):
        loads[i].wait()
    steps = [step_s[t] for t in range(TB)]
    places = []
    for t in range(TB):
        rank = jnp.int32(0)
        for before in range(t):
            rank = rank + jnp.where(steps[before] == steps[t], 1, 0)
        places.append(steps[t] * CAP + rank)
    source_of, slot_of = [], []
    for p in range(NWIN * CAP):
        t_of, slot_p = jnp.int32(0), jnp.int32(-1)
        for t in range(TB):
            t_of = jnp.where(places[t] == p, t, t_of)
            slot_p = jnp.where(places[t] == p, slot_s[t], slot_p)
        source_of.append(t_of)
        slot_of.append(slot_p)
    row = lax.broadcasted_iota(jnp.int32, (8, LANES), 0)
    for index in range(NWIN):
        tile = jnp.full((8, LANES), -1, jnp.int32)
        for rank in range(CAP):
            tile = jnp.where(row == rank, slot_of[index * CAP + rank], tile)
        slots_v[index] = tile

    def owner_copy(src, dst, which, index):
        return pltpu.make_async_remote_copy(
            src_ref=src, dst_ref=dst,
            send_sem=usend_sem.at[which, index], recv_sem=urecv_sem.at[which, index],
            device_id=(a, owner(index)), device_id_type=MESH,
        )

    slot_copies = [owner_copy(slots_v.at[i], slots_g.at[i], len(CHUNKS), i) for i in OFFSETS]
    for copy in slot_copies:
        copy.start()
    for i in range(4, 8):
        loads[i].wait()

    unit_copies = []
    for chunk, segment in enumerate(CHUNKS):
        for copy in pieces[chunk]:
            copy.wait_recv()
        low, high = segment * SEG, (segment + 1) * SEG
        for b in range(NSB):
            parts = [recv[chunk, b * 4 + s].astype(jnp.float32) for s in range(4)]
            groups = []
            for r in range(4):
                mixed = pick(quarter, [parts[(q - r) % 4] for q in range(4)])
                groups.append(pltpu.roll(mixed, (4 - r) * Q, 1) if r else mixed)
            coupler[b, low:high, :] = jnp.concatenate(groups, axis=0).astype(jnp.bfloat16)
        near_high, bil_low = min(high, HALF), max(low, HALF)
        fields = SEG // SUB

        def targets():
            for t in range(TB):
                lane = slice(t * BLK, (t + 1) * BLK)
                parts = []
                if low < near_high:
                    cells = coupler[near_s[t], low:near_high, :]
                    parts.append(jnp.dot(cells, near_wv[t], preferred_element_type=jnp.float32))
                if bil_low < high:
                    cells = jnp.concatenate(
                        [coupler[bil_s[k, t], bil_low:high, :] for k in range(NBIL)], axis=1
                    )
                    weights = bil_wv[t].reshape(NBIL * BLK, BLK)
                    parts.append(jnp.dot(cells, weights, preferred_element_type=jnp.float32))
                at = 0
                for part in parts:
                    full_v[t, low + at:low + at + part.shape[0], :] = part
                    remapped[low + at:low + at + part.shape[0], lane] = part.astype(jnp.bfloat16)
                    at += part.shape[0]
                total = full_v[t, pl.ds(low, fields, stride=SUB), :]
                for s in range(1, SUB):
                    total = total + full_v[t, pl.ds(low + s, fields, stride=SUB), :]
                units_v[t, low // SUB:high // SUB, :] = (total * (1.0 / SUB)).astype(jnp.bfloat16)

        targets()
        for index in (*OFFSETS, REACH):
            for rank in range(CAP):
                pack[chunk, index, rank] = units_v[source_of[index * CAP + rank], low // SUB:high // SUB, :]
        copies = [owner_copy(pack.at[chunk, i], got.at[chunk, i], chunk, i) for i in OFFSETS]
        for copy in copies:
            copy.start()
        unit_copies.append(copies)

    for copy in slot_copies:
        copy.wait_recv()
    for chunk, segment in enumerate(CHUNKS):
        low = segment * GRP
        for stage, indices in enumerate(((2, 1, 3), (0, 4))):
            for copy, index in zip(unit_copies[chunk], OFFSETS):
                if index in indices:
                    copy.wait_recv()
            for first in range(0, OWN_BLK, UNROLL):
                wanted = range(first, first + UNROLL)
                sums = [total_v[i] if stage else jnp.zeros((GRP, LANES), jnp.float32) for i in wanted]
                for index in indices:
                    mine = index == REACH
                    for rank in range(CAP):
                        unit = (pack if mine else got)[chunk, index, rank].astype(jnp.float32)
                        where = (slots_v if mine else slots_g)[index, rank:rank + 1, :]
                        where = jnp.broadcast_to(where, (GRP, LANES))
                        for j, i in enumerate(wanted):
                            sums[j] = sums[j] + jnp.where(where == i, unit, 0.0)
                for j, i in enumerate(wanted):
                    if stage:
                        ocean[i, low:low + GRP, :] = sums[j].astype(jnp.bfloat16)
                    else:
                        total_v[i] = sums[j]

    for group in (*pieces, *unit_copies, slot_copies):
        for copy in group:
            copy.wait_send()


def write(remapped, ocean, remapped_out, ocean_out, sem):
    copies = [
        pltpu.make_async_copy(remapped, remapped_out, sem.at[0]),
        pltpu.make_async_copy(ocean, ocean_out, sem.at[1]),
    ]
    for copy in copies:
        copy.start()
    for copy in copies:
        copy.wait()


def local(phys_flux, send_order, near_src, bil_src, nearest_w, bilinear_w, owner_step, slot):
    bf16, f32, i32 = jnp.bfloat16, jnp.float32, jnp.int32
    fields, chunks = ROWS // SUB, len(CHUNKS)
    dma = pltpu.SemaphoreType.DMA
    hbm = pl.BlockSpec(memory_space=pltpu.HBM)
    vmem = pl.BlockSpec(memory_space=pltpu.VMEM)
    args = (
        phys_flux, send_order, near_src, bil_src.T, nearest_w, bilinear_w, owner_step.reshape(TB), slot
    )
    results = pl.pallas_call(
        kernel,
        out_shape=(
            pltpu.VMEM((ROWS, TB * BLK), bf16),
            pltpu.VMEM((OWN_BLK, fields, BLK), bf16),
        ),
        in_specs=[hbm] * 8,
        out_specs=(vmem, vmem),
        scratch_shapes=[
            pltpu.VMEM((ROWS, COLS), bf16),
            pltpu.VMEM((1, COLS), i32),
            pltpu.VMEM((COLS, COLS), bf16),
            pltpu.VMEM((TB, BLK, BLK), bf16),
            pltpu.VMEM((TB, NBIL, BLK, BLK), bf16),
            pltpu.SMEM((TB,), i32),
            pltpu.SMEM((NBIL, TB), i32),
            pltpu.SMEM((TB,), i32),
            pltpu.SMEM((TB,), i32),
            pltpu.VMEM((chunks, N_ATM, GRP, LANES), bf16),
            pltpu.VMEM((chunks, N_ATM, GRP, LANES), bf16),
            pltpu.VMEM((NSB, ROWS, BLK), bf16),
            pltpu.VMEM((TB, ROWS, BLK), f32),
            pltpu.VMEM((TB, fields, BLK), bf16),
            pltpu.VMEM((chunks, NWIN, CAP, GRP, LANES), bf16),
            pltpu.VMEM((chunks, NWIN, CAP, GRP, LANES), bf16),
            pltpu.VMEM((NWIN, 8, LANES), i32),
            pltpu.VMEM((NWIN, 8, LANES), i32),
            pltpu.VMEM((OWN_BLK, GRP, LANES), f32),
            dma((8,)),
            dma((chunks, N_ATM)),
            dma((chunks, N_ATM)),
            dma((chunks + 1, NWIN)),
            dma((chunks + 1, NWIN)),
        ],
        compiler_params=pltpu.CompilerParams(
            collective_id=0, has_side_effects=True, vmem_limit_bytes=24 << 20
        ),
        name="coupler",
    )(*[pltpu.with_memory_space_constraint(x, pltpu.HBM) for x in args])
    return pl.pallas_call(
        write,
        out_shape=(
            pltpu.HBM((ROWS, TB * BLK), bf16),
            pltpu.HBM((OWN_BLK, fields, BLK), bf16),
        ),
        in_specs=[vmem, vmem],
        out_specs=(hbm, hbm),
        scratch_shapes=[dma((2,))],
        compiler_params=pltpu.CompilerParams(vmem_limit_bytes=1 << 20),
        name="write",
    )(*[pltpu.with_memory_space_constraint(x, pltpu.VMEM) for x in results])


def solution(mesh):
    placed = (
        P(None, ("atm", "ocn")),
        P(("atm", "ocn"), None),
        P(("atm", "ocn")),
        P(("atm", "ocn"), None),
        P(("atm", "ocn"), None, None),
        P(("atm", "ocn"), None, None, None),
        P(("atm", "ocn"), None),
        P(("atm", "ocn")),
    )
    return jax.shard_map(
        local,
        mesh=mesh,
        in_specs=placed,
        out_specs=(P(None, ("atm", "ocn")), P(("atm", "ocn"), None, None)),
        check_vma=False,
    )
```
